512 devices in a mesh: gx: 16 (over y, core), gy: 32 (over x, z).
Axes of the slice: x: 4, y: 8, z: 8, core: 2. Of those that a mesh axis runs over, the one named last changes fastest.
Arguments:
- dens_pres: float32 [2, 128, 512, 128], P(None, 'gx', 'gy'), may hold values from 0.7 to 1.3
- velocity: float32 [3, 128, 512, 128], P(None, 'gx', 'gy'), may hold values from -0.9 to 0.9
- cut_class: int32 [128, 512, 128], P('gx', 'gy'), may hold values from 0 to 3
- nbhd_cells: int32 [16, 32, 32, 64], P('gx', 'gy'), may hold values from 0 to 16383, as said below
- helper_list: int32 [16, 32, 32], P('gx', 'gy'), may hold values from 0 to 31, as said below
- live_counts: int32 [16, 32], P('gx', 'gy'), may hold values from 16 to 32, as said below
- redist_weights: float32 [16, 32, 32, 2, 64, 64], P('gx', 'gy'), may hold values from -0.2 to 0.7
Outputs:
- new_state: float32 [5, 128, 512, 128], P(None, 'gx', 'gy')
The draws below stay inside these ranges and needn't reach their ends.
Inputs may be any that keep to these rules, and one draw needn't show every extreme that they name: `nbhd_cells`: in each grid block the 32 x 64 entries are distinct cell numbers of that block. `helper_list`: in each grid block no helper is named by more than 2 slots, and at least one helper is named by exactly 2. `live_counts`: the slots below the count are live.
All inputs are finite; a program needn't handle non-finite values.
Results may differ from the reference program's by a relative error of at most 0.0003.
Values sent between devices are 32-bit elements; how exact they have to be, the bound alone decides.
No kernel may reach another device: no remote copies, remote signals or barrier semaphores. Data moves between devices by JAX's collectives and lax.ppermute only.
A program may use at most 64 MiB of HBM per device.

```python
import jax
import jax.numpy as jnp
from jax import lax

CX = 8
CY = 16
NZ = 128
NBR = 64
NB_DEV = 32
CAP = 2
NX = 128
NY = 512
N_GX = 16
N_GY = 32


def draw_nbhd_cells(key, part):
    keys = jax.random.split(key, N_GX * N_GY)

    def single(subkey):
        order = jax.random.permutation(subkey, CX * CY * NZ)
        return order[:NB_DEV * NBR].reshape(NB_DEV, NBR).astype(jnp.int32)
    return jax.vmap(single)(keys).reshape(N_GX, N_GY, NB_DEV, NBR)


def draw_helper_list(key, part):
    keys = jax.random.split(key, N_GX * N_GY)
    base_pool = jnp.repeat(jnp.arange(N_GY, dtype=jnp.int32), CAP)

    def single(subkey):
        first_key, second_key, third_key = jax.random.split(subkey, 3)
        leader = jax.random.randint(first_key, (), 0, N_GY)
        rolled = jnp.roll(base_pool, -leader * CAP)
        others = jax.random.permutation(second_key, rolled[CAP:])
        listed = jnp.concatenate([rolled[:CAP], others])[:NB_DEV]
        return jax.random.permutation(third_key, listed).astype(jnp.int32)
    return jax.vmap(single)(keys).reshape(N_GX, N_GY, NB_DEV)


def draw_live_counts(key, part):
    total = N_GX * N_GY
    first_key, second_key, third_key = jax.random.split(key, 3)
    counts = jax.random.randint(first_key, (total,), NB_DEV // 2, NB_DEV + 1)
    fullest = jax.random.randint(second_key, (), 0, total)
    emptiest = (fullest + 1 + jax.random.randint(third_key, (), 0, total - 1)) % total
    counts = counts.at[fullest].set(NB_DEV).at[emptiest].set(NB_DEV // 2)
    return counts.reshape(N_GX, N_GY).astype(jnp.int32)


def draw_redist_weights(key, part):
    shape = (N_GX, N_GY, N_GY, CAP, NBR, NBR)
    spread = jnp.clip(jax.random.normal(key, shape, jnp.float32), -4.0, 4.0) * 0.05
    rows = lax.broadcasted_iota(jnp.int32, shape, 4)
    columns = lax.broadcasted_iota(jnp.int32, shape, 5)
    return spread + jnp.where(rows == columns, 0.5, 0.0).astype(jnp.float32)


def set_ends(result, stream_key, smallest, largest):
    place = [jax.random.randint(jax.random.fold_in(stream_key, axis), (), 0, length) for axis, length in enumerate(result.shape)]
    longest = result.shape.index(max(result.shape))
    next_to = place[:longest] + [(place[longest] + 1) % result.shape[longest]] + place[longest + 1:]
    return result.at[tuple(place)].set(smallest).at[tuple(next_to)].set(largest)


def shard_levels(key, extent, shards, least, top_value):
    factor_of, own = 1.0, jax.random.fold_in(key, 6)
    for position, shards_of in shards:
        heights = jnp.exp(jax.random.uniform(jax.random.fold_in(own, position), (shards_of,), jnp.float32, least / len(shards), top_value / len(shards)))
        factor_of = factor_of * jnp.repeat(heights, extent[position] // shards_of).reshape([-1 if axis == position else 1 for axis in range(len(extent))])
    return factor_of


def gaussian(stream_key, extent, scale, most, shards=(), kind=jnp.bfloat16):
    factor_of = shard_levels(stream_key, extent, shards, -0.22, 0.18) if shards else 1.0
    drawn = jax.random.normal(stream_key, extent, jnp.float32) * scale * factor_of
    return jnp.minimum(jnp.maximum(drawn, -most), most).astype(kind)


def setup_inputs(seed: int = 0) -> dict:
    streams_of = jax.random.split(jax.random.key(seed), 8)
    dens_pres = jnp.clip(0.7 + 0.59999996 * jax.random.uniform(streams_of[0], (2, NX, NY, NZ), jnp.float32) ** shard_levels(streams_of[0], (2, NX, NY, NZ), ((1, 16), (2, 32)), -0.2, 0.2), 0.7, 1.3)
    velocity = gaussian(streams_of[1], (3, NX, NY, NZ), 0.3, 0.9, ((1, 16), (2, 32)), jnp.float32)
    cut_class = set_ends(jax.random.randint(streams_of[2], (NX, NY, NZ), 0, 4), jax.random.fold_in(streams_of[2], 1), 0, 3).astype(jnp.int32)
    nbhd_cells = draw_nbhd_cells(jax.random.fold_in(streams_of[7], 71), 0)
    helper_list = draw_helper_list(jax.random.fold_in(streams_of[7], 71), 0)
    live_counts = draw_live_counts(jax.random.fold_in(streams_of[7], 71), 0)
    redist_weights = draw_redist_weights(jax.random.fold_in(streams_of[7], 71), 0)
    return {"dens_pres": dens_pres, "velocity": velocity, "cut_class": cut_class, "nbhd_cells": nbhd_cells, "helper_list": helper_list, "live_counts": live_counts, "redist_weights": redist_weights}


GAS_GAMMA = 1.4
STEP_RATIO = 0.3

def minmod(lower_diff, upper_diff):
    return 0.5 * (jnp.sign(lower_diff) + jnp.sign(upper_diff)) * jnp.minimum(jnp.abs(lower_diff), jnp.abs(upper_diff))

def conserved(primitive):
    density = primitive[0]
    speeds = primitive[1:4]
    pressure = primitive[4]
    energy = pressure / (GAS_GAMMA - 1.0) + 0.5 * density * lax.optimization_barrier(jnp.sum(speeds * speeds, axis=0))
    return jnp.concatenate([density[None], density[None] * speeds, energy[None]], axis=0)

def face_flux(primitive, normal):
    density = primitive[0]
    pressure = primitive[4]
    normal_speed = primitive[1 + normal]
    state = conserved(primitive)
    flux = state * normal_speed[None]
    flux = flux.at[1 + normal].add(pressure)
    flux = flux.at[4].add(pressure * normal_speed)
    sound = jnp.sqrt(GAS_GAMMA * pressure / density)
    return (state, flux, jnp.abs(normal_speed) + sound)

def rusanov(lower_state, upper_state, normal):
    cons_low, flux_low, speed_low = face_flux(lower_state, normal)
    cons_up, flux_up, speed_up = face_flux(upper_state, normal)
    wave = jnp.maximum(speed_low, speed_up)
    return 0.5 * (flux_low + flux_up) - 0.5 * wave[None] * (cons_up - cons_low)

def piece(array, start, stop, axis):
    return lax.slice_in_dim(array, start, stop, axis=axis)

def divergence(padded, normal):
    axis = normal + 1
    length = padded.shape[axis] - 4
    jumps = piece(padded, 1, length + 4, axis) - piece(padded, 0, length + 3, axis)
    slopes = minmod(piece(jumps, 0, length + 2, axis), piece(jumps, 1, length + 3, axis))
    centres = piece(padded, 1, length + 3, axis)
    lower_state = piece(centres, 0, length + 1, axis) + 0.5 * piece(slopes, 0, length + 1, axis)
    upper_state = piece(centres, 1, length + 2, axis) - 0.5 * piece(slopes, 1, length + 2, axis)
    fluxes = rusanov(lower_state, upper_state, normal)
    return piece(fluxes, 1, length + 1, axis) - piece(fluxes, 0, length, axis)

def wrap_pad(array, axis):
    widths = [(0, 0)] * array.ndim
    widths[axis] = (2, 2)
    return jnp.pad(array, widths, mode='wrap')

def slot_ranks(helper_row):
    count = helper_row.shape[0]
    same = helper_row[None, :] == helper_row[:, None]
    lower = lax.broadcasted_iota(jnp.int32, (count, count), 1) < lax.broadcasted_iota(jnp.int32, (count, count), 0)
    return lax.optimization_barrier(jnp.sum((same & lower).astype(jnp.int32), axis=1)).astype(jnp.int32)

def reference(dens_pres, velocity, cut_class, nbhd_cells, helper_list, live_counts, redist_weights):
    primitive = jnp.concatenate([dens_pres[0:1], velocity, dens_pres[1:2]], axis=0)
    total_div = divergence(wrap_pad(primitive, 1), 0)
    total_div = total_div + divergence(wrap_pad(primitive, 2), 1)
    total_div = total_div + divergence(wrap_pad(primitive, 3), 2)
    kappa = 0.25 * (1.0 + cut_class.astype(jnp.float32))
    delta = -STEP_RATIO * total_div / kappa[None]
    blocks = delta.reshape(5, N_GX, CX, N_GY, CY, NZ).transpose(1, 3, 0, 2, 4, 5).reshape(N_GX, N_GY, 5, CX * CY * NZ)
    column_ids = jnp.arange(N_GY, dtype=jnp.int32)

    def per_group(inputs):
        block_row, cell_row, helper_row, count_row, weight_row = inputs

        def per_block(block, cells, helpers, count, column):
            ranks = slot_ranks(helpers)
            values = block[:, cells]
            chosen = weight_row[helpers, column, ranks]
            mixed = jnp.einsum('nij,vnj->vni', chosen, values, precision=lax.Precision.HIGHEST)
            live = jnp.arange(NB_DEV, dtype=jnp.int32) < count
            mixed = jnp.where(live[None, :, None], mixed, values)
            return block.at[:, cells.reshape(-1)].set(mixed.reshape(5, -1))
        return jax.vmap(per_block)(block_row, cell_row, helper_row, count_row, column_ids)
    blocks = lax.map(per_group, (blocks, nbhd_cells, helper_list, live_counts, redist_weights))
    delta = blocks.reshape(N_GX, N_GY, 5, CX, CY, NZ).transpose(2, 0, 3, 1, 4, 5).reshape(5, N_GX * CX, N_GY * CY, NZ)
    return conserved(primitive) + delta
```

```python
import jax
import jax.numpy as jnp
from jax import lax
from jax.experimental import pallas as pl
from jax.experimental.pallas import tpu as pltpu
from jax.sharding import PartitionSpec as P

GAS_GAMMA = 1.4
STEP_RATIO = 0.3
F32 = jnp.float32
BF16 = jnp.bfloat16
VMEM_SPEC = pl.BlockSpec(memory_space=pltpu.VMEM)
SMEM_SPEC = pl.BlockSpec(memory_space=pltpu.SMEM)


def halo_kernel(dp_ref, vel_ref, xhead_ref, xtail_ref, yhead_ref, ytail_ref):
    nx, ny = dp_ref.shape[1], dp_ref.shape[2]
    for comp in range(5):
        ref, k = (vel_ref, comp - 1) if 1 <= comp <= 3 else (dp_ref, comp // 4)
        xhead_ref[comp] = ref[k, 0:2]
        xtail_ref[comp] = ref[k, nx - 2 : nx]
        for x in range(nx):
            row = (comp * nx + x) * 2
            yhead_ref[row : row + 2, :] = ref[k, x, 0:2, :]
            ytail_ref[row : row + 2, :] = ref[k, x, ny - 2 : ny, :]


def pack_halo(dens_pres, velocity):
    _, nx, ny, nz = dens_pres.shape
    xs = jax.ShapeDtypeStruct((5, 2, ny, nz), F32)
    ys = jax.ShapeDtypeStruct((5 * nx * 2, nz), F32)
    return pl.pallas_call(
        halo_kernel,
        out_shape=(xs, xs, ys, ys),
        in_specs=[VMEM_SPEC] * 2,
        out_specs=(VMEM_SPEC,) * 4,
        name="halo_pack",
    )(dens_pres, velocity)


def weight_kernel(w_ref, o_ref):
    o_ref[...] = jnp.concatenate([w_ref[:, 0], w_ref[:, 1]], axis=-1)


def pack_weights(weights):
    blocks, cap, n, _ = weights.shape
    step = 8
    return pl.pallas_call(
        weight_kernel,
        out_shape=jax.ShapeDtypeStruct((blocks, n, cap * n), F32),
        grid=(blocks // step,),
        in_specs=[pl.BlockSpec((step, cap, n, n), lambda i: (i, 0, 0, 0))],
        out_specs=pl.BlockSpec((step, n, cap * n), lambda i: (i, 0, 0)),
        name="weight_pack",
    )(weights)


def minmod(a, b):
    return jnp.maximum(jnp.minimum(a, b), 0.0) + jnp.minimum(jnp.maximum(a, b), 0.0)


def cons_of(p):
    rho, u, v, w, pr = p
    ke = u * u + v * v + w * w
    return [rho, rho * u, rho * v, rho * w, pr * (1.0 / (GAS_GAMMA - 1.0)) + 0.5 * rho * ke]


def face_parts(p, n):
    cons = cons_of(p)
    un, pr = p[1 + n], p[4]
    flux = [c * un for c in cons]
    flux[1 + n] = flux[1 + n] + pr
    flux[4] = flux[4] + pr * un
    gp = GAS_GAMMA * pr
    speed = jnp.abs(un) + gp * lax.rsqrt(gp * p[0])
    return cons, flux, speed


def rusanov2(low, up, n):
    c0, f0, s0 = face_parts(low, n)
    c1, f1, s1 = face_parts(up, n)
    wave = jnp.maximum(s0, s1)
    return [(f0[i] + f1[i]) - wave * (c1[i] - c0[i]) for i in range(5)]


def rolled_divergence(p, axis, n):
    length = p[0].shape[axis]

    def back(v):
        return pltpu.roll(v, 1, axis)

    def ahead(v):
        return pltpu.roll(v, length - 1, axis)

    low, up = [], []
    for v in p:
        d = v - back(v)
        half = 0.5 * minmod(d, ahead(d))
        low.append(v + half)
        up.append(ahead(v - half))
    flux = rusanov2(low, up, n)
    return [f - back(f) for f in flux]


def cell_parts(c):
    row = (c >> 11) * 8 + ((c >> 7) & 7)
    lane = ((c >> 10) & 1) * 128 + (c & 127)
    return row, lane


def one_hot(ids, size):
    width = ids.shape[1]
    return lax.broadcasted_iota(jnp.int32, (size, width), 0) == ids


def flux_kernel(
    rank_ref, dp_ref, vel_ref, cut_ref, xlo_ref, xhi_ref, ylo_ref, yhi_ref, cell_ref,
    base_ref, val_ref, lhs_ref, xe, ye, dl,
):
    nx = dp_ref.shape[1]
    for comp in range(5):
        ref, k = (vel_ref, comp - 1) if 1 <= comp <= 3 else (dp_ref, comp // 4)
        xe[comp, 0:2] = xlo_ref[comp]
        xe[comp, 2 : nx + 2] = ref[k]
        xe[comp, nx + 2 : nx + 4] = xhi_ref[comp]
        for x in range(nx):
            row = (comp * nx + x) * 2
            ye[comp, x, 0:2, :] = ylo_ref[row : row + 2, :]
            ye[comp, x, 2:18, :] = ref[k, x]
            ye[comp, x, 18:20, :] = yhi_ref[row : row + 2, :]
            ye[comp, x, 20:24, :] = ref[k, x, 0:4, :]

    def plane(j):
        return [xe[c, j] for c in range(5)]

    def face_x(j):
        a, b, c, d = plane(j - 1), plane(j), plane(j + 1), plane(j + 2)
        low, up = [], []
        for i in range(5):
            mid = c[i] - b[i]
            low.append(b[i] + 0.5 * minmod(b[i] - a[i], mid))
            up.append(c[i] - 0.5 * minmod(mid, d[i] - c[i]))
        return rusanov2(low, up, 0)

    def body(x, before):
        after = face_x(x + 2)
        ydiv = rolled_divergence([ye[c, x] for c in range(5)], 0, 1)
        centre = plane(x + 2)
        zdiv = rolled_divergence(centre, 1, 2)
        kappa4 = 1.0 + cut_ref[x].astype(F32)
        scale = (-2.0 * STEP_RATIO) / kappa4
        cons = cons_of(centre)
        for i in range(5):
            delta = scale * ((after[i] - before[i]) + zdiv[i] + ydiv[i][2:18])
            base_ref[i, x] = cons[i] + delta
            row = pl.multiple_of(i * 64 + x * 8, 8)
            dl[pl.ds(row, 8), 0:128] = delta[0:8]
            dl[pl.ds(row, 8), 128:256] = delta[8:16]
        return after

    lax.fori_loop(0, nx, body, face_x(1))

    whole = dl[...]
    hi = whole.astype(BF16)
    rest = whole - hi.astype(F32)
    mid = rest.astype(BF16)
    low = (rest - mid.astype(F32)).astype(BF16)
    pieces = jnp.concatenate([hi, mid, low], axis=0)
    half_id = lax.broadcasted_iota(jnp.int32, (8, 128), 1) // 64
    for q in range(8):
        row, lane = cell_parts(cell_ref[q : q + 1, :])
        lane_hot = one_hot(lane, 256).astype(F32).astype(BF16)
        got = jnp.dot(pieces, lane_hot, preferred_element_type=F32)
        got = got[0:320] + (got[320:640] + got[640:960])
        row_hot = one_hot(row, 64)
        rows = [
            jnp.sum(jnp.where(row_hot, got[v * 64 : v * 64 + 64], 0.0), axis=0, keepdims=True)
            for v in range(5)
        ]
        val = jnp.concatenate(rows + [jnp.zeros((3, 256), F32)], axis=0)
        val_ref[q] = val
        placed = []
        for t in range(4):
            part = val[:, (t // 2) * 128 : (t // 2) * 128 + 128]
            rank = rank_ref[q * 4 + t]
            moved = jnp.where(rank == t % 2, part, pltpu.roll(part, 64, 1))
            placed.append(jnp.where(half_id == rank, moved, 0.0))
        x = jnp.concatenate(placed, axis=0)
        x_hi = x.astype(BF16)
        x_lo = (x - x_hi.astype(F32)).astype(BF16)
        both = jnp.concatenate([x_hi, x_lo], axis=0)
        lhs_ref[q] = jnp.concatenate([both, both], axis=1)


def fluxes(ranks, dens_pres, velocity, cut_class, xlo, xhi, ylo, yhi, cells):
    _, nx, ny, nz = dens_pres.shape
    return pl.pallas_call(
        flux_kernel,
        out_shape=(
            jax.ShapeDtypeStruct((5, nx, ny, nz), F32),
            jax.ShapeDtypeStruct((8, 8, 256), F32),
            jax.ShapeDtypeStruct((8, 64, 256), BF16),
        ),
        in_specs=[SMEM_SPEC] + [VMEM_SPEC] * 8,
        out_specs=(VMEM_SPEC,) * 3,
        scratch_shapes=[
            pltpu.VMEM((5, nx + 4, ny, nz), F32),
            pltpu.VMEM((5, nx, 24, nz), F32),
            pltpu.VMEM((320, 256), F32),
        ],
        name="flux_gather",
    )(ranks, dens_pres, velocity, cut_class, xlo, xhi, ylo, yhi, cells)


def contract_last(a, b):
    return lax.dot_general(a, b, (((1,), (1,)), ((), ())), preferred_element_type=F32)


def mix_kernel(helper_ref, live_ref, w_ref, lhs_ref, val_ref, cell_ref, base_ref, out_ref):
    nx = base_ref.shape[1]
    live = live_ref[0]
    slot_of = lax.broadcasted_iota(jnp.int32, (8, 256), 1) // 64
    total = jnp.zeros((320, 256), F32)
    for q in range(8):
        tiles = []
        for t in range(4):
            w = w_ref[helper_ref[q * 4 + t]]
            w_hi = w.astype(BF16)
            w_lo = (w - w_hi.astype(F32)).astype(BF16)
            tiles.append(jnp.concatenate([w_hi, w_lo], axis=1))
        made = contract_last(lhs_ref[q], jnp.concatenate(tiles, axis=0))
        made = made[0:32] + made[32:64]
        mixed = made[0:8]
        for t in range(1, 4):
            mixed = jnp.where(slot_of == t, made[t * 8 : t * 8 + 8], mixed)
        diff = jnp.where(q * 4 + slot_of < live, mixed - val_ref[q], 0.0)
        d_hi = diff.astype(BF16).astype(F32)
        d_lo = diff - d_hi
        row, lane = cell_parts(cell_ref[q : q + 1, :])
        row_hot = one_hot(row, 64)
        lane_hot = one_hot(lane, 256).astype(F32).astype(BF16)
        spread = [
            jnp.concatenate(
                [jnp.where(row_hot, d[v : v + 1, :], 0.0).astype(BF16) for v in range(5)], axis=0
            )
            for d in (d_hi, d_lo)
        ]
        total = total + contract_last(spread[0], lane_hot) + contract_last(spread[1], lane_hot)
    for v in range(5):
        for x in range(nx):
            row = v * 64 + x * 8
            out_ref[v, x, 0:8, :] = base_ref[v, x, 0:8, :] + total[row : row + 8, 0:128]
            out_ref[v, x, 8:16, :] = base_ref[v, x, 8:16, :] + total[row : row + 8, 128:256]


def redistribute(helpers, live, weights, lhs, val, cells, base):
    return pl.pallas_call(
        mix_kernel,
        out_shape=jax.ShapeDtypeStruct(base.shape, F32),
        in_specs=[SMEM_SPEC] * 2 + [VMEM_SPEC] * 5,
        out_specs=VMEM_SPEC,
        name="mix_scatter",
    )(helpers, live, weights, lhs, val, cells, base)


def local(dens_pres, velocity, cut_class, nbhd_cells, helper_list, live_counts, redist_weights):
    ngx, ngy = lax.axis_size("gx"), lax.axis_size("gy")
    packed = pack_weights(redist_weights[0, 0])
    weights = lax.all_to_all(packed, "gy", split_axis=0, concat_axis=0, tiled=True)
    xhead, xtail, yhead, ytail = pack_halo(dens_pres, velocity)
    up_x = [(i, (i + 1) % ngx) for i in range(ngx)]
    up_y = [(i, (i + 1) % ngy) for i in range(ngy)]
    ylo = lax.ppermute(ytail, "gy", up_y)
    yhi = lax.ppermute(yhead, "gy", [(b, a) for a, b in up_y])
    xlo = lax.ppermute(xtail, "gx", up_x)
    xhi = lax.ppermute(xhead, "gx", [(b, a) for a, b in up_x])
    helpers = helper_list[0, 0]
    slots = helpers.shape[0]
    same = helpers[None, :] == helpers[:, None]
    below = lax.broadcasted_iota(jnp.int32, (slots, slots), 1) < lax.broadcasted_iota(
        jnp.int32, (slots, slots), 0
    )
    ranks = jnp.sum((same & below).astype(jnp.int32), axis=1)
    cells = nbhd_cells.reshape(8, 256)
    base, val, lhs = fluxes(
        ranks, dens_pres, velocity, cut_class, xlo, xhi, ylo, yhi, cells
    )
    return redistribute(helpers, live_counts[0], weights, lhs, val, cells, base)


def solution(mesh):
    in_specs = (
        P(None, "gx", "gy", None),
        P(None, "gx", "gy", None),
        P("gx", "gy", None),
        P("gx", "gy", None, None),
        P("gx", "gy", None),
        P("gx", "gy"),
        P("gx", "gy", None, None, None, None),
    )
    out_specs = P(None, "gx", "gy", None)
    return jax.shard_map(local, mesh=mesh, in_specs=in_specs, out_specs=out_specs, check_vma=False)
```

```python
import jax
import jax.numpy as jnp
from jax import lax
from jax.experimental import pallas as pl
from jax.experimental.pallas import tpu as pltpu
from jax.sharding import PartitionSpec as P

GAS_GAMMA = 1.4
STEP_RATIO = 0.3
F32 = jnp.float32
BF16 = jnp.bfloat16
VMEM_SPEC = pl.BlockSpec(memory_space=pltpu.VMEM)
SMEM_SPEC = pl.BlockSpec(memory_space=pltpu.SMEM)
ANY_SPEC = pl.BlockSpec(memory_space=pl.ANY)
PARAMS = pltpu.CompilerParams(vmem_limit_bytes=16 << 20)


def comp_ref(dp_ref, vel_ref, comp):
    return (vel_ref, comp - 1) if 1 <= comp <= 3 else (dp_ref, comp // 4)


def halo_kernel(dp_ref, vel_ref, xhead_ref, xtail_ref, yhead_ref, ytail_ref):
    for comp in range(5):
        ref, k = comp_ref(dp_ref, vel_ref, comp)
        xhead_ref[comp] = ref[k, 0:32, :]
        xtail_ref[comp] = ref[k, 96:128, :]
        for j in range(2):
            row = comp * 16 + j * 8
            yhead_ref[row : row + 8, :] = ref[k, pl.ds(j, 8, stride=16), :]
            ytail_ref[row : row + 8, :] = ref[k, pl.ds(14 + j, 8, stride=16), :]


def pack_halo(dens_pres, velocity):
    xs = jax.ShapeDtypeStruct((5, 32, 128), F32)
    ys = jax.ShapeDtypeStruct((80, 128), F32)
    return pl.pallas_call(
        halo_kernel,
        out_shape=(xs, xs, ys, ys),
        in_specs=[VMEM_SPEC] * 2,
        out_specs=(VMEM_SPEC,) * 4,
        compiler_params=PARAMS,
        name="halo_pack",
    )(dens_pres, velocity)


def weight_kernel(w_ref, o_ref, held, packed, in_sems, out_sems):
    chunks = in_sems.shape[0]
    step = w_ref.shape[0] // chunks

    def part(c):
        return pl.ds(c * step, step)

    def load(c):
        return pltpu.make_async_copy(w_ref.at[part(c)], held.at[part(c)], in_sems.at[c])

    def store(c):
        return pltpu.make_async_copy(packed.at[part(c)], o_ref.at[part(c)], out_sems.at[c])

    for c in range(chunks):
        load(c).start()
    for c in range(chunks):
        load(c).wait()
        packed[part(c)] = jnp.concatenate([held[part(c), 0], held[part(c), 1]], axis=-1)
        store(c).start()
    for c in range(chunks):
        store(c).wait()


def pack_weights(weights):
    blocks, cap, n, _ = weights.shape
    return pl.pallas_call(
        weight_kernel,
        out_shape=jax.ShapeDtypeStruct((blocks, n, cap * n), F32),
        in_specs=[ANY_SPEC],
        out_specs=ANY_SPEC,
        scratch_shapes=[
            pltpu.VMEM(weights.shape, F32),
            pltpu.VMEM((blocks, n, cap * n), F32),
            pltpu.SemaphoreType.DMA((8,)),
            pltpu.SemaphoreType.DMA((8,)),
        ],
        compiler_params=pltpu.CompilerParams(vmem_limit_bytes=60 << 20),
        name="weight_pack",
    )(weights)


def minmod(a, b):
    return jnp.maximum(jnp.minimum(a, b), 0.0) + jnp.minimum(jnp.maximum(a, b), 0.0)


def cons_of(p):
    rho, u, v, w, pr = p
    ke = u * u + v * v + w * w
    return [rho, rho * u, rho * v, rho * w, pr * (1.0 / (GAS_GAMMA - 1.0)) + 0.5 * rho * ke]


def face_parts(p, n):
    cons = cons_of(p)
    un, pr = p[1 + n], p[4]
    flux = [c * un for c in cons]
    flux[1 + n] = flux[1 + n] + pr
    flux[4] = flux[4] + pr * un
    gp = GAS_GAMMA * pr
    speed = jnp.abs(un) + gp * lax.rsqrt(gp * p[0])
    return cons, flux, speed


def rusanov2(low, up, n):
    c0, f0, s0 = face_parts(low, n)
    c1, f1, s1 = face_parts(up, n)
    wave = jnp.maximum(s0, s1)
    return [(f0[i] + f1[i]) - wave * (c1[i] - c0[i]) for i in range(5)]


def rolled_divergence(p, axis, n, keep=None):
    length = p[0].shape[axis]

    def back(v):
        return pltpu.roll(v, 1, axis)

    def ahead(v):
        return pltpu.roll(v, length - 1, axis)

    low, up = [], []
    for v in p:
        d = v - back(v)
        half = 0.5 * minmod(d, ahead(d))
        low.append(v + half)
        up.append(ahead(v - half))
    flux = rusanov2(low, up, n)
    if keep is not None:
        flux = [jnp.where(keep, f, 0.0) for f in flux]
    return [f - back(f) for f in flux]


def cell_parts(c):
    row = (c >> 11) * 8 + ((c >> 7) & 7)
    lane = ((c >> 10) & 1) * 128 + (c & 127)
    return row, lane


def one_hot(ids, size):
    width = ids.shape[1]
    return lax.broadcasted_iota(jnp.int32, (size, width), 0) == ids


def two_parts(v):
    hi = v.astype(BF16)
    return hi, (v - hi.astype(F32)).astype(BF16)


def flux_kernel(
    dp_ref, vel_ref, cut_ref, xlo_ref, xhi_ref, cell_ref, base_ref, val_ref, edge_ref, scale_ref,
    xe, dl,
):
    for comp in range(5):
        ref, k = comp_ref(dp_ref, vel_ref, comp)
        xe[comp, 0:32] = xlo_ref[comp]
        xe[comp, 32:160] = ref[k]
        xe[comp, 160:192] = xhi_ref[comp]
        for j, row in enumerate((0, 1, 2, 13, 14, 15)):
            edge_ref[comp, j] = ref[k, pl.ds(row, 8, stride=16), :]
    for j, row in enumerate((0, 1, 14, 15)):
        cut = cut_ref[pl.ds(row, 8, stride=16), :].astype(F32)
        scale_ref[j] = (-2.0 * STEP_RATIO) / (1.0 + cut)

    def plane(j):
        return [xe[c, pl.ds(pl.multiple_of(j * 16, 16), 16), :] for c in range(5)]

    def face_x(j):
        a, b, c, d = plane(j - 1), plane(j), plane(j + 1), plane(j + 2)
        low, up = [], []
        for i in range(5):
            mid = c[i] - b[i]
            low.append(b[i] + 0.5 * minmod(b[i] - a[i], mid))
            up.append(c[i] - 0.5 * minmod(mid, d[i] - c[i]))
        return rusanov2(low, up, 0)

    row_id = lax.broadcasted_iota(jnp.int32, (16, 128), 0)
    inner = (row_id >= 1) & (row_id <= 13)

    def body(x, before):
        after = face_x(x + 2)
        centre = plane(x + 2)
        ydiv = rolled_divergence(centre, 0, 1, inner)
        zdiv = rolled_divergence(centre, 1, 2)
        here = pl.ds(pl.multiple_of(x * 16, 16), 16)
        scale = (-2.0 * STEP_RATIO) / (1.0 + cut_ref[here, :].astype(F32))
        cons = cons_of(centre)
        for i in range(5):
            delta = scale * ((after[i] - before[i]) + zdiv[i] + ydiv[i])
            base_ref[i, here, :] = cons[i] + delta
            row = pl.multiple_of(i * 64 + x * 8, 8)
            dl[pl.ds(row, 8), 0:128] = delta[0:8]
            dl[pl.ds(row, 8), 128:256] = delta[8:16]
        return after

    lax.fori_loop(0, 8, body, face_x(1))

    whole = dl[...]
    hi = whole.astype(BF16)
    rest = whole - hi.astype(F32)
    mid, low = two_parts(rest)
    pieces = jnp.concatenate([hi, mid, low], axis=0)
    for q in range(8):
        row, lane = cell_parts(cell_ref[q : q + 1, :])
        lane_hot = one_hot(lane, 256).astype(F32).astype(BF16)
        got = jnp.dot(pieces, lane_hot, preferred_element_type=F32)
        got = got[0:320] + (got[320:640] + got[640:960])
        row_hot = one_hot(row, 64)
        rows = [
            jnp.sum(jnp.where(row_hot, got[v * 64 : v * 64 + 64], 0.0), axis=0, keepdims=True)
            for v in range(5)
        ]
        val_ref[q] = jnp.concatenate(rows + [jnp.zeros((3, 256), F32)], axis=0)


def fluxes(dens_pres, velocity, cut_class, xlo, xhi, cells):
    return pl.pallas_call(
        flux_kernel,
        out_shape=(
            jax.ShapeDtypeStruct((5, 128, 128), F32),
            jax.ShapeDtypeStruct((8, 8, 256), F32),
            jax.ShapeDtypeStruct((5, 6, 8, 128), F32),
            jax.ShapeDtypeStruct((4, 8, 128), F32),
        ),
        in_specs=[VMEM_SPEC] * 6,
        out_specs=(VMEM_SPEC,) * 4,
        scratch_shapes=[pltpu.VMEM((5, 192, 128), F32), pltpu.VMEM((320, 256), F32)],
        compiler_params=PARAMS,
        name="flux_gather",
    )(dens_pres, velocity, cut_class, xlo, xhi, cells)


def edge_kernel(
    rank_ref, edge_ref, scale_ref, ylo_ref, yhi_ref, cell_ref, part_ref, fix_ref, val_ref, lhs_ref
):
    def halo(ref, j):
        return [ref[c * 16 + j * 8 : c * 16 + j * 8 + 8, :] for c in range(5)]

    def own(j):
        return [edge_ref[c, j] for c in range(5)]

    def two_faces(rows):
        low, up = [], []
        for k in (1, 2, 3):
            half = [
                0.5 * minmod(rows[k][c] - rows[k - 1][c], rows[k + 1][c] - rows[k][c])
                for c in range(5)
            ]
            low.append([rows[k][c] + half[c] for c in range(5)])
            up.append([rows[k][c] - half[c] for c in range(5)])
        return rusanov2(low[0], up[1], 1), rusanov2(low[1], up[2], 1)

    face_a, face_b = two_faces([halo(ylo_ref, 0), halo(ylo_ref, 1), own(0), own(1), own(2)])
    face_c, face_d = two_faces([own(3), own(4), own(5), halo(yhi_ref, 0), halo(yhi_ref, 1)])
    fix = []
    for c in range(5):
        fix.append(
            [
                scale_ref[0] * (face_b[c] - face_a[c]),
                -scale_ref[1] * face_b[c],
                scale_ref[2] * face_c[c],
                scale_ref[3] * (face_d[c] - face_c[c]),
            ]
        )
        for j in range(4):
            fix_ref[c, j] = fix[c][j]
    table = jnp.concatenate(
        [
            jnp.concatenate([fix[c][j], fix[c][j + 2]], axis=1)
            for c in range(5)
            for j in range(2)
        ],
        axis=0,
    )
    pieces = jnp.concatenate(two_parts(table), axis=0)
    half_id = lax.broadcasted_iota(jnp.int32, (8, 128), 1) // 64
    for q in range(8):
        cell = cell_ref[q : q + 1, :]
        x, y, z = cell >> 11, (cell >> 7) & 15, cell & 127
        on_edge = (y < 2) | (y > 13)
        row = jnp.where(on_edge, (y & 1) * 8 + x, -1)
        lane = (y >> 3) * 128 + z
        got = jnp.dot(pieces, one_hot(lane, 256).astype(F32).astype(BF16), preferred_element_type=F32)
        got = got[0:80] + got[80:160]
        row_hot = one_hot(row, 16)
        rows = [
            jnp.sum(jnp.where(row_hot, got[c * 16 : c * 16 + 16], 0.0), axis=0, keepdims=True)
            for c in range(5)
        ]
        val = part_ref[q] + jnp.concatenate(rows + [jnp.zeros((3, 256), F32)], axis=0)
        val_ref[q] = val
        placed = []
        for t in range(4):
            piece = val[:, (t // 2) * 128 : (t // 2) * 128 + 128]
            rank = rank_ref[q * 4 + t]
            moved = jnp.where(rank == t % 2, piece, pltpu.roll(piece, 64, 1))
            placed.append(jnp.where(half_id == rank, moved, 0.0))
        both = jnp.concatenate(two_parts(jnp.concatenate(placed, axis=0)), axis=0)
        lhs_ref[q] = jnp.concatenate([both, both], axis=1)


def edges(ranks, edge, scale, ylo, yhi, cells, part):
    return pl.pallas_call(
        edge_kernel,
        out_shape=(
            jax.ShapeDtypeStruct((5, 4, 8, 128), F32),
            jax.ShapeDtypeStruct((8, 8, 256), F32),
            jax.ShapeDtypeStruct((8, 64, 256), BF16),
        ),
        in_specs=[SMEM_SPEC] + [VMEM_SPEC] * 6,
        out_specs=(VMEM_SPEC,) * 3,
        compiler_params=PARAMS,
        name="edge_gather",
    )(ranks, edge, scale, ylo, yhi, cells, part)


def contract_last(a, b):
    return lax.dot_general(a, b, (((1,), (1,)), ((), ())), preferred_element_type=F32)


def mix_kernel(
    helper_ref, live_ref, w_ref, lhs_ref, val_ref, cell_ref, base_ref, fix_ref, out_ref
):
    live = live_ref[0]
    slot_of = lax.broadcasted_iota(jnp.int32, (8, 256), 1) // 64
    total = jnp.zeros((320, 256), F32)
    for q in range(8):
        tiles = []
        for t in range(4):
            w_hi, w_lo = two_parts(w_ref[helper_ref[q * 4 + t]])
            tiles.append(jnp.concatenate([w_hi, w_lo], axis=1))
        made = contract_last(lhs_ref[q], jnp.concatenate(tiles, axis=0))
        made = made[0:32] + made[32:64]
        mixed = made[0:8]
        for t in range(1, 4):
            mixed = jnp.where(slot_of == t, made[t * 8 : t * 8 + 8], mixed)
        diff = jnp.where(q * 4 + slot_of < live, mixed - val_ref[q], 0.0)
        d_hi = diff.astype(BF16).astype(F32)
        d_lo = diff - d_hi
        row, lane = cell_parts(cell_ref[q : q + 1, :])
        row_hot = one_hot(row, 64)
        lane_hot = one_hot(lane, 256).astype(F32).astype(BF16)
        spread = [
            jnp.concatenate(
                [jnp.where(row_hot, d[v : v + 1, :], 0.0).astype(BF16) for v in range(5)], axis=0
            )
            for d in (d_hi, d_lo)
        ]
        total = total + contract_last(spread[0], lane_hot) + contract_last(spread[1], lane_hot)
    for v in range(5):
        for x in range(8):
            row = v * 64 + x * 8
            top = slice(x * 16, x * 16 + 8)
            bottom = slice(x * 16 + 8, x * 16 + 16)
            out_ref[v, top, :] = base_ref[v, top, :] + total[row : row + 8, 0:128]
            out_ref[v, bottom, :] = base_ref[v, bottom, :] + total[row : row + 8, 128:256]
        for j, y in enumerate((0, 1, 14, 15)):
            rows = pl.ds(y, 8, stride=16)
            out_ref[v, rows, :] = out_ref[v, rows, :] + fix_ref[v, j]


def redistribute(helpers, live, weights, lhs, val, cells, base, fix):
    return pl.pallas_call(
        mix_kernel,
        out_shape=jax.ShapeDtypeStruct(base.shape, F32),
        in_specs=[SMEM_SPEC] * 2 + [VMEM_SPEC] * 6,
        out_specs=VMEM_SPEC,
        compiler_params=PARAMS,
        name="mix_scatter",
    )(helpers, live, weights, lhs, val, cells, base, fix)


def local(dens_pres, velocity, cut_class, nbhd_cells, helper_list, live_counts, redist_weights):
    ngx, ngy = lax.axis_size("gx"), lax.axis_size("gy")
    dens_pres = dens_pres.reshape(2, 128, 128)
    velocity = velocity.reshape(3, 128, 128)
    cut_class = cut_class.reshape(128, 128)
    packed = pack_weights(redist_weights[0, 0])
    weights = lax.all_to_all(packed, "gy", split_axis=0, concat_axis=0, tiled=True)
    xhead, xtail, yhead, ytail = pack_halo(dens_pres, velocity)
    up_x = [(i, (i + 1) % ngx) for i in range(ngx)]
    up_y = [(i, (i + 1) % ngy) for i in range(ngy)]
    ylo = lax.ppermute(ytail, "gy", up_y)
    yhi = lax.ppermute(yhead, "gy", [(b, a) for a, b in up_y])
    xlo = lax.ppermute(xtail, "gx", up_x)
    xhi = lax.ppermute(xhead, "gx", [(b, a) for a, b in up_x])
    helpers = helper_list[0, 0]
    slots = helpers.shape[0]
    same = helpers[None, :] == helpers[:, None]
    below = lax.broadcasted_iota(jnp.int32, (slots, slots), 1) < lax.broadcasted_iota(
        jnp.int32, (slots, slots), 0
    )
    ranks = jnp.sum((same & below).astype(jnp.int32), axis=1)
    cells = nbhd_cells.reshape(8, 256)
    base, part, edge, scale = fluxes(dens_pres, velocity, cut_class, xlo, xhi, cells)
    fix, val, lhs = edges(ranks, edge, scale, ylo, yhi, cells, part)
    out = redistribute(helpers, live_counts[0], weights, lhs, val, cells, base, fix)
    return out.reshape(5, 8, 16, 128)


def solution(mesh):
    in_specs = (
        P(None, "gx", "gy", None),
        P(None, "gx", "gy", None),
        P("gx", "gy", None),
        P("gx", "gy", None, None),
        P("gx", "gy", None),
        P("gx", "gy"),
        P("gx", "gy", None, None, None, None),
    )
    out_specs = P(None, "gx", "gy", None)
    return jax.shard_map(local, mesh=mesh, in_specs=in_specs, out_specs=out_specs, check_vma=False)
```

```python
import jax
import jax.numpy as jnp
from jax import lax
from jax.experimental import pallas as pl
from jax.experimental.pallas import tpu as pltpu
from jax.sharding import PartitionSpec as P

GAS_GAMMA = 1.4
STEP_RATIO = 0.3
F32 = jnp.float32
BF16 = jnp.bfloat16
VMEM_SPEC = pl.BlockSpec(memory_space=pltpu.VMEM)
SMEM_SPEC = pl.BlockSpec(memory_space=pltpu.SMEM)
ANY_SPEC = pl.BlockSpec(memory_space=pl.ANY)
PARAMS = pltpu.CompilerParams(vmem_limit_bytes=16 << 20)


def comp_ref(dp_ref, vel_ref, comp):
    return (vel_ref, comp - 1) if 1 <= comp <= 3 else (dp_ref, comp // 4)


def halo_kernel(dp_ref, vel_ref, xhead_ref, xtail_ref, yhead_ref, ytail_ref):
    for comp in range(5):
        ref, k = comp_ref(dp_ref, vel_ref, comp)
        xhead_ref[comp] = ref[k, 0:32, :]
        xtail_ref[comp] = ref[k, 96:128, :]
        for j in range(2):
            row = comp * 16 + j * 8
            yhead_ref[row : row + 8, :] = ref[k, pl.ds(j, 8, stride=16), :]
            ytail_ref[row : row + 8, :] = ref[k, pl.ds(14 + j, 8, stride=16), :]


def pack_halo(dens_pres, velocity):
    xs = jax.ShapeDtypeStruct((5, 32, 128), F32)
    ys = jax.ShapeDtypeStruct((80, 128), F32)
    return pl.pallas_call(
        halo_kernel,
        out_shape=(xs, xs, ys, ys),
        in_specs=[VMEM_SPEC] * 2,
        out_specs=(VMEM_SPEC,) * 4,
        compiler_params=PARAMS,
        name="halo_pack",
    )(dens_pres, velocity)


def weight_kernel(w_ref, o_ref, held, packed, in_sems, out_sems):
    chunks = in_sems.shape[0]
    step = w_ref.shape[0] // chunks

    def part(c):
        return pl.ds(c * step, step)

    def load(c):
        return pltpu.make_async_copy(w_ref.at[part(c)], held.at[part(c)], in_sems.at[c])

    def store(c):
        return pltpu.make_async_copy(packed.at[part(c)], o_ref.at[part(c)], out_sems.at[c])

    for c in range(chunks):
        load(c).start()
    for c in range(chunks):
        load(c).wait()
        packed[part(c)] = jnp.concatenate([held[part(c), 0], held[part(c), 1]], axis=-1)
        store(c).start()
    for c in range(chunks):
        store(c).wait()


def pack_weights(weights):
    blocks, cap, n, _ = weights.shape
    return pl.pallas_call(
        weight_kernel,
        out_shape=jax.ShapeDtypeStruct((blocks, n, cap * n), F32),
        in_specs=[ANY_SPEC],
        out_specs=ANY_SPEC,
        scratch_shapes=[
            pltpu.VMEM(weights.shape, F32),
            pltpu.VMEM((blocks, n, cap * n), F32),
            pltpu.SemaphoreType.DMA((4,)),
            pltpu.SemaphoreType.DMA((4,)),
        ],
        compiler_params=pltpu.CompilerParams(vmem_limit_bytes=60 << 20),
        name="weight_pack",
    )(weights)


def minmod(a, b):
    return jnp.maximum(jnp.minimum(a, b), 0.0) + jnp.minimum(jnp.maximum(a, b), 0.0)


def cons_of(p):
    rho, u, v, w, pr = p
    ke = u * u + v * v + w * w
    return [rho, rho * u, rho * v, rho * w, pr * (1.0 / (GAS_GAMMA - 1.0)) + 0.5 * rho * ke]


def face_parts(p, n):
    cons = cons_of(p)
    un, pr = p[1 + n], p[4]
    flux = [c * un for c in cons]
    flux[1 + n] = flux[1 + n] + pr
    flux[4] = flux[4] + pr * un
    gp = GAS_GAMMA * pr
    speed = jnp.abs(un) + gp * lax.rsqrt(gp * p[0])
    return cons, flux, speed


def rusanov2(low, up, n):
    c0, f0, s0 = face_parts(low, n)
    c1, f1, s1 = face_parts(up, n)
    wave = jnp.maximum(s0, s1)
    return [(f0[i] + f1[i]) - wave * (c1[i] - c0[i]) for i in range(5)]


def rolled_divergence(p, axis, n, keep=None):
    length = p[0].shape[axis]

    def back(v):
        return pltpu.roll(v, 1, axis)

    def ahead(v):
        return pltpu.roll(v, length - 1, axis)

    low, up = [], []
    for v in p:
        d = v - back(v)
        half = 0.5 * minmod(d, ahead(d))
        low.append(v + half)
        up.append(ahead(v - half))
    flux = rusanov2(low, up, n)
    if keep is not None:
        flux = [jnp.where(keep, f, 0.0) for f in flux]
    return [f - back(f) for f in flux]


def cell_parts(c):
    row = (c >> 11) * 8 + ((c >> 7) & 7)
    lane = ((c >> 10) & 1) * 128 + (c & 127)
    return row, lane


def one_hot(ids, size):
    width = ids.shape[1]
    return lax.broadcasted_iota(jnp.int32, (size, width), 0) == ids


def two_parts(v):
    hi = v.astype(BF16)
    return hi, (v - hi.astype(F32)).astype(BF16)


def flux_kernel(
    rank_ref, live_ref, dp_ref, vel_ref, cut_ref, xlo_ref, xhi_ref, cell_ref,
    base_ref, val_ref, edge_ref, scale_ref, half_ref, live_out_ref, xe, dl,
):
    for s in range(32):
        half_ref[s : s + 1, :] = jnp.full((1, 128), rank_ref[s], jnp.int32)
    slot = lax.broadcasted_iota(jnp.int32, (8, 256), 0) * 4
    slot = slot + lax.broadcasted_iota(jnp.int32, (8, 256), 1) // 64
    live_out_ref[...] = jnp.where(slot < live_ref[0], 1.0, 0.0)
    for comp in range(5):
        ref, k = comp_ref(dp_ref, vel_ref, comp)
        xe[comp, 0:32] = xlo_ref[comp]
        xe[comp, 32:160] = ref[k]
        xe[comp, 160:192] = xhi_ref[comp]
        for j, row in enumerate((0, 1, 2, 13, 14, 15)):
            edge_ref[comp, j] = ref[k, pl.ds(row, 8, stride=16), :]
    for j, row in enumerate((0, 1, 14, 15)):
        cut = cut_ref[pl.ds(row, 8, stride=16), :].astype(F32)
        scale_ref[j] = (-2.0 * STEP_RATIO) / (1.0 + cut)

    def plane(j):
        return [xe[c, pl.ds(pl.multiple_of(j * 16, 16), 16), :] for c in range(5)]

    def face_x(j):
        a, b, c, d = plane(j - 1), plane(j), plane(j + 1), plane(j + 2)
        low, up = [], []
        for i in range(5):
            mid = c[i] - b[i]
            low.append(b[i] + 0.5 * minmod(b[i] - a[i], mid))
            up.append(c[i] - 0.5 * minmod(mid, d[i] - c[i]))
        return rusanov2(low, up, 0)

    row_id = lax.broadcasted_iota(jnp.int32, (16, 128), 0)
    inner = (row_id >= 1) & (row_id <= 13)

    def body(x, before):
        after = face_x(x + 2)
        centre = plane(x + 2)
        ydiv = rolled_divergence(centre, 0, 1, inner)
        zdiv = rolled_divergence(centre, 1, 2)
        here = pl.ds(pl.multiple_of(x * 16, 16), 16)
        scale = (-2.0 * STEP_RATIO) / (1.0 + cut_ref[here, :].astype(F32))
        cons = cons_of(centre)
        for i in range(5):
            delta = scale * ((after[i] - before[i]) + zdiv[i] + ydiv[i])
            base_ref[i, here, :] = cons[i] + delta
            row = pl.multiple_of(i * 64 + x * 8, 8)
            dl[pl.ds(row, 8), 0:128] = delta[0:8]
            dl[pl.ds(row, 8), 128:256] = delta[8:16]
        return after

    lax.fori_loop(0, 8, body, face_x(1))

    whole = dl[...]
    hi = whole.astype(BF16)
    rest = whole - hi.astype(F32)
    mid, low = two_parts(rest)
    pieces = jnp.concatenate([hi, mid, low], axis=0)
    for q in range(8):
        row, lane = cell_parts(cell_ref[q : q + 1, :])
        lane_hot = one_hot(lane, 256).astype(F32).astype(BF16)
        got = jnp.dot(pieces, lane_hot, preferred_element_type=F32)
        got = got[0:320] + (got[320:640] + got[640:960])
        row_hot = one_hot(row, 64)
        rows = [
            jnp.sum(jnp.where(row_hot, got[v * 64 : v * 64 + 64], 0.0), axis=0, keepdims=True)
            for v in range(5)
        ]
        val_ref[q] = jnp.concatenate(rows + [jnp.zeros((3, 256), F32)], axis=0)


def fluxes(ranks, live, dens_pres, velocity, cut_class, xlo, xhi, cells):
    return pl.pallas_call(
        flux_kernel,
        out_shape=(
            jax.ShapeDtypeStruct((5, 128, 128), F32),
            jax.ShapeDtypeStruct((8, 8, 256), F32),
            jax.ShapeDtypeStruct((5, 6, 8, 128), F32),
            jax.ShapeDtypeStruct((4, 8, 128), F32),
            jax.ShapeDtypeStruct((32, 128), jnp.int32),
            jax.ShapeDtypeStruct((8, 256), F32),
        ),
        in_specs=[SMEM_SPEC] * 2 + [VMEM_SPEC] * 6,
        out_specs=(VMEM_SPEC,) * 6,
        scratch_shapes=[pltpu.VMEM((5, 192, 128), F32), pltpu.VMEM((320, 256), F32)],
        compiler_params=PARAMS,
        name="flux_gather",
    )(ranks, live, dens_pres, velocity, cut_class, xlo, xhi, cells)


def edge_kernel(
    half_ref, live_ref, edge_ref, scale_ref, ylo_ref, yhi_ref, cell_ref, part_ref,
    fix_ref, val_ref, lhs_ref,
):
    def halo(ref, j):
        return [ref[c * 16 + j * 8 : c * 16 + j * 8 + 8, :] for c in range(5)]

    def own(j):
        return [edge_ref[c, j] for c in range(5)]

    def two_faces(rows):
        low, up = [], []
        for k in (1, 2, 3):
            half = [
                0.5 * minmod(rows[k][c] - rows[k - 1][c], rows[k + 1][c] - rows[k][c])
                for c in range(5)
            ]
            low.append([rows[k][c] + half[c] for c in range(5)])
            up.append([rows[k][c] - half[c] for c in range(5)])
        return rusanov2(low[0], up[1], 1), rusanov2(low[1], up[2], 1)

    face_a, face_b = two_faces([halo(ylo_ref, 0), halo(ylo_ref, 1), own(0), own(1), own(2)])
    face_c, face_d = two_faces([own(3), own(4), own(5), halo(yhi_ref, 0), halo(yhi_ref, 1)])
    fix = []
    for c in range(5):
        fix.append(
            [
                scale_ref[0] * (face_b[c] - face_a[c]),
                -scale_ref[1] * face_b[c],
                scale_ref[2] * face_c[c],
                scale_ref[3] * (face_d[c] - face_c[c]),
            ]
        )
        for j in range(4):
            fix_ref[c, j] = fix[c][j]
    table = jnp.concatenate(
        [
            jnp.concatenate([fix[c][j], fix[c][j + 2]], axis=1)
            for c in range(5)
            for j in range(2)
        ],
        axis=0,
    )
    pieces = jnp.concatenate(two_parts(table), axis=0)
    half_id = lax.broadcasted_iota(jnp.int32, (8, 128), 1) // 64
    for q in range(8):
        cell = cell_ref[q : q + 1, :]
        x, y, z = cell >> 11, (cell >> 7) & 15, cell & 127
        on_edge = (y < 2) | (y > 13)
        row = jnp.where(on_edge, (y & 1) * 8 + x, -1)
        lane = (y >> 3) * 128 + z
        got = jnp.dot(pieces, one_hot(lane, 256).astype(F32).astype(BF16), preferred_element_type=F32)
        got = got[0:80] + got[80:160]
        row_hot = one_hot(row, 16)
        rows = [
            jnp.sum(jnp.where(row_hot, got[c * 16 : c * 16 + 16], 0.0), axis=0, keepdims=True)
            for c in range(5)
        ]
        val = part_ref[q] + jnp.concatenate(rows + [jnp.zeros((3, 256), F32)], axis=0)
        val = jnp.where(live_ref[q : q + 1, :] > 0.0, val, 0.0)
        val_ref[q] = val
        placed = []
        for t in range(4):
            piece = val[:, (t // 2) * 128 : (t // 2) * 128 + 128]
            rank = half_ref[q * 4 + t : q * 4 + t + 1, :]
            moved = jnp.where(rank == t % 2, piece, pltpu.roll(piece, 64, 1))
            placed.append(jnp.where(half_id == rank, moved, 0.0))
        both = jnp.concatenate(two_parts(jnp.concatenate(placed, axis=0)), axis=0)
        lhs_ref[q] = jnp.concatenate([both, both], axis=1)


def edges(half, live, edge, scale, ylo, yhi, cells, part):
    return pl.pallas_call(
        edge_kernel,
        out_shape=(
            jax.ShapeDtypeStruct((5, 4, 8, 128), F32),
            jax.ShapeDtypeStruct((8, 8, 256), F32),
            jax.ShapeDtypeStruct((8, 64, 256), BF16),
        ),
        in_specs=[VMEM_SPEC] * 8,
        out_specs=(VMEM_SPEC,) * 3,
        compiler_params=PARAMS,
        name="edge_gather",
    )(half, live, edge, scale, ylo, yhi, cells, part)


def contract_last(a, b):
    return lax.dot_general(a, b, (((1,), (1,)), ((), ())), preferred_element_type=F32)


def mix_kernel(
    helper_ref, w_ref, lhs_ref, val_ref, cell_ref, base_ref, fix_ref, out_ref,
    helper, made, helper_sem, out_sems,
):
    fetch = pltpu.make_async_copy(helper_ref, helper, helper_sem)
    fetch.start()
    slot_of = lax.broadcasted_iota(jnp.int32, (8, 256), 1) // 64
    lane_hots, row_hots = [], []
    for q in range(8):
        row, lane = cell_parts(cell_ref[q : q + 1, :])
        row_hots.append(one_hot(row, 64))
        lane_hots.append(one_hot(lane, 256).astype(F32).astype(BF16))
    fetch.wait()
    diffs = []
    for q in range(8):
        tiles = []
        for t in range(4):
            w_hi, w_lo = two_parts(w_ref[helper[q * 4 + t]])
            tiles.append(jnp.concatenate([w_hi, w_lo], axis=1))
        got = contract_last(lhs_ref[q], jnp.concatenate(tiles, axis=0))
        got = got[0:32] + got[32:64]
        mixed = got[0:8]
        for t in range(1, 4):
            mixed = jnp.where(slot_of == t, got[t * 8 : t * 8 + 8], mixed)
        diffs.append(mixed - val_ref[q])
    columns = []
    for q in range(8):
        d_hi = diffs[q].astype(BF16).astype(F32)
        spread = [
            jnp.where(row_hots[q], d[v : v + 1, :], 0.0).astype(BF16)
            for d in (d_hi, diffs[q] - d_hi)
            for v in range(5)
        ]
        columns.append(jnp.concatenate(spread, axis=0))
    both = contract_last(jnp.concatenate(columns, axis=1), jnp.concatenate(lane_hots, axis=1))
    total = both[0:320] + both[320:640]

    def store(v):
        return pltpu.make_async_copy(made.at[v], out_ref.at[v], out_sems.at[v])

    for v in range(5):
        for x in range(8):
            row = v * 64 + x * 8
            top = slice(x * 16, x * 16 + 8)
            bottom = slice(x * 16 + 8, x * 16 + 16)
            made[v, top, :] = base_ref[v, top, :] + total[row : row + 8, 0:128]
            made[v, bottom, :] = base_ref[v, bottom, :] + total[row : row + 8, 128:256]
        for j, y in enumerate((0, 1, 14, 15)):
            rows = pl.ds(y, 8, stride=16)
            made[v, rows, :] = made[v, rows, :] + fix_ref[v, j]
        store(v).start()
    for v in range(5):
        store(v).wait()


def redistribute(helpers, weights, lhs, val, cells, base, fix):
    return pl.pallas_call(
        mix_kernel,
        out_shape=jax.ShapeDtypeStruct(base.shape, F32),
        in_specs=[ANY_SPEC] + [VMEM_SPEC] * 6,
        out_specs=ANY_SPEC,
        scratch_shapes=[
            pltpu.SMEM((32,), jnp.int32),
            pltpu.VMEM((5, 128, 128), F32),
            pltpu.SemaphoreType.DMA,
            pltpu.SemaphoreType.DMA((5,)),
        ],
        compiler_params=PARAMS,
        name="mix_scatter",
    )(helpers, weights, lhs, val, cells, base, fix)


def local(dens_pres, velocity, cut_class, nbhd_cells, helper_list, live_counts, redist_weights):
    ngx, ngy = lax.axis_size("gx"), lax.axis_size("gy")
    dens_pres = dens_pres.reshape(2, 128, 128)
    velocity = velocity.reshape(3, 128, 128)
    cut_class = cut_class.reshape(128, 128)
    packed = pack_weights(redist_weights[0, 0])
    weights = lax.all_to_all(packed, "gy", split_axis=0, concat_axis=0, tiled=True)
    xhead, xtail, yhead, ytail = pack_halo(dens_pres, velocity)
    up_x = [(i, (i + 1) % ngx) for i in range(ngx)]
    up_y = [(i, (i + 1) % ngy) for i in range(ngy)]
    ylo = lax.ppermute(ytail, "gy", up_y)
    yhi = lax.ppermute(yhead, "gy", [(b, a) for a, b in up_y])
    xlo = lax.ppermute(xtail, "gx", up_x)
    xhi = lax.ppermute(xhead, "gx", [(b, a) for a, b in up_x])
    helpers = helper_list[0, 0]
    slots = helpers.shape[0]
    same = helpers[None, :] == helpers[:, None]
    below = lax.broadcasted_iota(jnp.int32, (slots, slots), 1) < lax.broadcasted_iota(
        jnp.int32, (slots, slots), 0
    )
    ranks = jnp.sum((same & below).astype(jnp.int32), axis=1)
    cells = nbhd_cells.reshape(8, 256)
    base, part, edge, scale, half, live = fluxes(
        ranks, live_counts[0], dens_pres, velocity, cut_class, xlo, xhi, cells
    )
    fix, val, lhs = edges(half, live, edge, scale, ylo, yhi, cells, part)
    out = redistribute(helpers, weights, lhs, val, cells, base, fix)
    return out.reshape(5, 8, 16, 128)


def solution(mesh):
    in_specs = (
        P(None, "gx", "gy", None),
        P(None, "gx", "gy", None),
        P("gx", "gy", None),
        P("gx", "gy", None, None),
        P("gx", "gy", None),
        P("gx", "gy"),
        P("gx", "gy", None, None, None, None),
    )
    out_specs = P(None, "gx", "gy", None)
    return jax.shard_map(local, mesh=mesh, in_specs=in_specs, out_specs=out_specs, check_vma=False)
```

```python
import jax
import jax.numpy as jnp
from jax import lax
from jax.experimental import pallas as pl
from jax.experimental.pallas import tpu as pltpu
from jax.sharding import PartitionSpec as P


GAS_GAMMA = 1.4
STEP_RATIO = 0.3
F32 = jnp.float32
BF16 = jnp.bfloat16
VMEM_SPEC = pl.BlockSpec(memory_space=pltpu.VMEM)
SMEM_SPEC = pl.BlockSpec(memory_space=pltpu.SMEM)
ANY_SPEC = pl.BlockSpec(memory_space=pl.ANY)
PARAMS = pltpu.CompilerParams(vmem_limit_bytes=16 << 20)


def comp_ref(dp_ref, vel_ref, comp):
    return (vel_ref, comp - 1) if 1 <= comp <= 3 else (dp_ref, comp // 4)


def halo_kernel(dp_ref, vel_ref, xhead_ref, xtail_ref, yhead_ref, ytail_ref):
    for comp in range(5):
        ref, k = comp_ref(dp_ref, vel_ref, comp)
        xhead_ref[comp] = ref[k, 0:32, :]
        xtail_ref[comp] = ref[k, 96:128, :]
        for j in range(2):
            row = comp * 16 + j * 8
            yhead_ref[row : row + 8, :] = ref[k, pl.ds(j, 8, stride=16), :]
            ytail_ref[row : row + 8, :] = ref[k, pl.ds(14 + j, 8, stride=16), :]


def pack_halo(dens_pres, velocity):
    xs = jax.ShapeDtypeStruct((5, 32, 128), F32)
    ys = jax.ShapeDtypeStruct((80, 128), F32)
    return pl.pallas_call(
        halo_kernel,
        out_shape=(xs, xs, ys, ys),
        in_specs=[VMEM_SPEC] * 2,
        out_specs=(VMEM_SPEC,) * 4,
        compiler_params=PARAMS,
        name="halo_pack",
    )(dens_pres, velocity)


def place_of(g):
    x, z = g >> 3, g & 7
    return (7 - z) * 4 + (x)


def columns_in_order(count):
    return sorted(range(count), key=place_of)


def weight_kernel(w_ref, o_ref, held, packed, in_sems, out_sems):
    chunks = in_sems.shape[0]
    depth = w_ref.shape[1] // chunks
    step = w_ref.shape[0] * depth
    order = columns_in_order(chunks * step)

    def load(c):
        part = pl.ds((chunks - 1 - c) * depth, depth)
        return pltpu.make_async_copy(w_ref.at[:, part], held.at[:, part], in_sems.at[c])

    def store(c):
        part = pl.ds(c * step, step)
        return pltpu.make_async_copy(packed.at[part], o_ref.at[part], out_sems.at[c])

    for c in range(chunks):
        load(c).start()
    for c in range(chunks):
        load(c).wait()
        for k in range(c * step, (c + 1) * step):
            x, z = order[k] >> 3, order[k] & 7
            packed[k] = jnp.concatenate([held[x, z, 0], held[x, z, 1]], axis=-1)
        store(c).start()
    for c in range(chunks):
        store(c).wait()


def pack_weights(weights):
    blocks, cap, n, _ = weights.shape
    weights = weights.reshape(4, 8, cap, n, n)
    return pl.pallas_call(
        weight_kernel,
        out_shape=jax.ShapeDtypeStruct((blocks, n, cap * n), F32),
        in_specs=[ANY_SPEC],
        out_specs=ANY_SPEC,
        scratch_shapes=[
            pltpu.VMEM(weights.shape, F32),
            pltpu.VMEM((blocks, n, cap * n), F32),
            pltpu.SemaphoreType.DMA((4,)),
            pltpu.SemaphoreType.DMA((4,)),
        ],
        compiler_params=pltpu.CompilerParams(vmem_limit_bytes=60 << 20),
        name="weight_pack",
    )(weights)


def minmod(a, b):
    return jnp.maximum(jnp.minimum(a, b), 0.0) + jnp.minimum(jnp.maximum(a, b), 0.0)


def cons_of(p):
    rho, u, v, w, pr = p
    ke = u * u + v * v + w * w
    return [rho, rho * u, rho * v, rho * w, pr * (1.0 / (GAS_GAMMA - 1.0)) + 0.5 * rho * ke]


def face_parts(p, n):
    cons = cons_of(p)
    un, pr = p[1 + n], p[4]
    flux = [c * un for c in cons]
    flux[1 + n] = flux[1 + n] + pr
    flux[4] = flux[4] + pr * un
    gp = GAS_GAMMA * pr
    speed = jnp.abs(un) + gp * lax.rsqrt(gp * p[0])
    return cons, flux, speed


def rusanov2(low, up, n):
    c0, f0, s0 = face_parts(low, n)
    c1, f1, s1 = face_parts(up, n)
    wave = jnp.maximum(s0, s1)
    return [(f0[i] + f1[i]) - wave * (c1[i] - c0[i]) for i in range(5)]


def rolled_divergence(p, axis, n, keep=None):
    length = p[0].shape[axis]

    def back(v):
        return pltpu.roll(v, 1, axis)

    def ahead(v):
        return pltpu.roll(v, length - 1, axis)

    low, up = [], []
    for v in p:
        d = v - back(v)
        half = 0.5 * minmod(d, ahead(d))
        low.append(v + half)
        up.append(ahead(v - half))
    flux = rusanov2(low, up, n)
    if keep is not None:
        flux = [jnp.where(keep, f, 0.0) for f in flux]
    return [f - back(f) for f in flux]


def cell_parts(c):
    row = (c >> 11) * 8 + ((c >> 7) & 7)
    lane = ((c >> 10) & 1) * 128 + (c & 127)
    return row, lane


def one_hot(ids, size):
    width = ids.shape[1]
    return lax.broadcasted_iota(jnp.int32, (size, width), 0) == ids


def two_parts(v):
    hi = v.astype(BF16)
    return hi, (v - hi.astype(F32)).astype(BF16)


def flux_kernel(
    rank_ref, live_ref, dp_ref, vel_ref, cut_ref, xlo_ref, xhi_ref, cell_ref,
    base_ref, val_ref, edge_ref, scale_ref, half_ref, live_out_ref, xe, dl,
):
    for s in range(32):
        half_ref[s : s + 1, :] = jnp.full((1, 128), rank_ref[s], jnp.int32)
    slot = lax.broadcasted_iota(jnp.int32, (8, 256), 0) * 4
    slot = slot + lax.broadcasted_iota(jnp.int32, (8, 256), 1) // 64
    live_out_ref[...] = jnp.where(slot < live_ref[0], 1.0, 0.0)
    for comp in range(5):
        ref, k = comp_ref(dp_ref, vel_ref, comp)
        xe[comp, 0:32] = xlo_ref[comp]
        xe[comp, 32:160] = ref[k]
        xe[comp, 160:192] = xhi_ref[comp]
        for j, row in enumerate((0, 1, 2, 13, 14, 15)):
            edge_ref[comp, j] = ref[k, pl.ds(row, 8, stride=16), :]
    for j, row in enumerate((0, 1, 14, 15)):
        cut = cut_ref[pl.ds(row, 8, stride=16), :].astype(F32)
        scale_ref[j] = (-2.0 * STEP_RATIO) / (1.0 + cut)

    def plane(j):
        return [xe[c, pl.ds(pl.multiple_of(j * 16, 16), 16), :] for c in range(5)]

    def face_x(j):
        a, b, c, d = plane(j - 1), plane(j), plane(j + 1), plane(j + 2)
        low, up = [], []
        for i in range(5):
            mid = c[i] - b[i]
            low.append(b[i] + 0.5 * minmod(b[i] - a[i], mid))
            up.append(c[i] - 0.5 * minmod(mid, d[i] - c[i]))
        return rusanov2(low, up, 0)

    row_id = lax.broadcasted_iota(jnp.int32, (16, 128), 0)
    inner = (row_id >= 1) & (row_id <= 13)

    def body(x, before):
        after = face_x(x + 2)
        centre = plane(x + 2)
        ydiv = rolled_divergence(centre, 0, 1, inner)
        zdiv = rolled_divergence(centre, 1, 2)
        here = pl.ds(pl.multiple_of(x * 16, 16), 16)
        scale = (-2.0 * STEP_RATIO) / (1.0 + cut_ref[here, :].astype(F32))
        cons = cons_of(centre)
        for i in range(5):
            delta = scale * ((after[i] - before[i]) + zdiv[i] + ydiv[i])
            base_ref[i, here, :] = cons[i] + delta
            row = pl.multiple_of(i * 64 + x * 8, 8)
            dl[pl.ds(row, 8), 0:128] = delta[0:8]
            dl[pl.ds(row, 8), 128:256] = delta[8:16]
        return after

    lax.fori_loop(0, 8, body, face_x(1))

    whole = dl[...]
    hi = whole.astype(BF16)
    rest = whole - hi.astype(F32)
    mid, low = two_parts(rest)
    pieces = jnp.concatenate([hi, mid, low], axis=0)
    for q in range(8):
        row, lane = cell_parts(cell_ref[q : q + 1, :])
        lane_hot = one_hot(lane, 256).astype(F32).astype(BF16)
        got = jnp.dot(pieces, lane_hot, preferred_element_type=F32)
        got = got[0:320] + (got[320:640] + got[640:960])
        row_hot = one_hot(row, 64)
        rows = [
            jnp.sum(jnp.where(row_hot, got[v * 64 : v * 64 + 64], 0.0), axis=0, keepdims=True)
            for v in range(5)
        ]
        val_ref[q] = jnp.concatenate(rows + [jnp.zeros((3, 256), F32)], axis=0)


def fluxes(ranks, live, dens_pres, velocity, cut_class, xlo, xhi, cells):
    return pl.pallas_call(
        flux_kernel,
        out_shape=(
            jax.ShapeDtypeStruct((5, 128, 128), F32),
            jax.ShapeDtypeStruct((8, 8, 256), F32),
            jax.ShapeDtypeStruct((5, 6, 8, 128), F32),
            jax.ShapeDtypeStruct((4, 8, 128), F32),
            jax.ShapeDtypeStruct((32, 128), jnp.int32),
            jax.ShapeDtypeStruct((8, 256), F32),
        ),
        in_specs=[SMEM_SPEC] * 2 + [VMEM_SPEC] * 6,
        out_specs=(VMEM_SPEC,) * 6,
        scratch_shapes=[pltpu.VMEM((5, 192, 128), F32), pltpu.VMEM((320, 256), F32)],
        compiler_params=PARAMS,
        name="flux_gather",
    )(ranks, live, dens_pres, velocity, cut_class, xlo, xhi, cells)


def edge_kernel(
    half_ref, live_ref, edge_ref, scale_ref, ylo_ref, yhi_ref, cell_ref, part_ref,
    fix_ref, val_ref, lhs_ref,
):
    def halo(ref, j):
        return [ref[c * 16 + j * 8 : c * 16 + j * 8 + 8, :] for c in range(5)]

    def own(j):
        return [edge_ref[c, j] for c in range(5)]

    def two_faces(rows):
        low, up = [], []
        for k in (1, 2, 3):
            half = [
                0.5 * minmod(rows[k][c] - rows[k - 1][c], rows[k + 1][c] - rows[k][c])
                for c in range(5)
            ]
            low.append([rows[k][c] + half[c] for c in range(5)])
            up.append([rows[k][c] - half[c] for c in range(5)])
        return rusanov2(low[0], up[1], 1), rusanov2(low[1], up[2], 1)

    face_a, face_b = two_faces([halo(ylo_ref, 0), halo(ylo_ref, 1), own(0), own(1), own(2)])
    face_c, face_d = two_faces([own(3), own(4), own(5), halo(yhi_ref, 0), halo(yhi_ref, 1)])
    fix = []
    for c in range(5):
        fix.append(
            [
                scale_ref[0] * (face_b[c] - face_a[c]),
                -scale_ref[1] * face_b[c],
                scale_ref[2] * face_c[c],
                scale_ref[3] * (face_d[c] - face_c[c]),
            ]
        )
        for j in range(4):
            fix_ref[c, j] = fix[c][j]
    table = jnp.concatenate(
        [
            jnp.concatenate([fix[c][j], fix[c][j + 2]], axis=1)
            for c in range(5)
            for j in range(2)
        ],
        axis=0,
    )
    pieces = jnp.concatenate(two_parts(table), axis=0)
    half_id = lax.broadcasted_iota(jnp.int32, (8, 128), 1) // 64
    for q in range(8):
        cell = cell_ref[q : q + 1, :]
        x, y, z = cell >> 11, (cell >> 7) & 15, cell & 127
        on_edge = (y < 2) | (y > 13)
        row = jnp.where(on_edge, (y & 1) * 8 + x, -1)
        lane = (y >> 3) * 128 + z
        got = jnp.dot(pieces, one_hot(lane, 256).astype(F32).astype(BF16), preferred_element_type=F32)
        got = got[0:80] + got[80:160]
        row_hot = one_hot(row, 16)
        rows = [
            jnp.sum(jnp.where(row_hot, got[c * 16 : c * 16 + 16], 0.0), axis=0, keepdims=True)
            for c in range(5)
        ]
        val = part_ref[q] + jnp.concatenate(rows + [jnp.zeros((3, 256), F32)], axis=0)
        val = jnp.where(live_ref[q : q + 1, :] > 0.0, val, 0.0)
        val_ref[q] = val
        placed = []
        for t in range(4):
            piece = val[:, (t // 2) * 128 : (t // 2) * 128 + 128]
            rank = half_ref[q * 4 + t : q * 4 + t + 1, :]
            moved = jnp.where(rank == t % 2, piece, pltpu.roll(piece, 64, 1))
            placed.append(jnp.where(half_id == rank, moved, 0.0))
        both = jnp.concatenate(two_parts(jnp.concatenate(placed, axis=0)), axis=0)
        lhs_ref[q] = jnp.concatenate([both, both], axis=1)


def edges(half, live, edge, scale, ylo, yhi, cells, part):
    return pl.pallas_call(
        edge_kernel,
        out_shape=(
            jax.ShapeDtypeStruct((5, 4, 8, 128), F32),
            jax.ShapeDtypeStruct((8, 8, 256), F32),
            jax.ShapeDtypeStruct((8, 64, 256), BF16),
        ),
        in_specs=[VMEM_SPEC] * 8,
        out_specs=(VMEM_SPEC,) * 3,
        compiler_params=PARAMS,
        name="edge_gather",
    )(half, live, edge, scale, ylo, yhi, cells, part)


def contract_last(a, b):
    return lax.dot_general(a, b, (((1,), (1,)), ((), ())), preferred_element_type=F32)


def mix_kernel(
    helper_ref, w_ref, lhs_ref, val_ref, cell_ref, base_ref, fix_ref, out_ref,
    helper, made, helper_sem, out_sems,
):
    fetch = pltpu.make_async_copy(helper_ref, helper, helper_sem)
    fetch.start()
    slot_of = lax.broadcasted_iota(jnp.int32, (8, 256), 1) // 64
    lane_hots, row_hots = [], []
    for q in range(8):
        row, lane = cell_parts(cell_ref[q : q + 1, :])
        row_hots.append(one_hot(row, 64))
        lane_hots.append(one_hot(lane, 256).astype(F32).astype(BF16))
    fetch.wait()
    diffs = []
    for q in range(8):
        tiles = []
        for t in range(4):
            w_hi, w_lo = two_parts(w_ref[place_of(helper[q * 4 + t])])
            tiles.append(jnp.concatenate([w_hi, w_lo], axis=1))
        got = contract_last(lhs_ref[q], jnp.concatenate(tiles, axis=0))
        got = got[0:32] + got[32:64]
        mixed = got[0:8]
        for t in range(1, 4):
            mixed = jnp.where(slot_of == t, got[t * 8 : t * 8 + 8], mixed)
        diffs.append(mixed - val_ref[q])
    columns = []
    for q in range(8):
        d_hi = diffs[q].astype(BF16).astype(F32)
        spread = [
            jnp.where(row_hots[q], d[v : v + 1, :], 0.0).astype(BF16)
            for d in (d_hi, diffs[q] - d_hi)
            for v in range(5)
        ]
        columns.append(jnp.concatenate(spread, axis=0))
    both = contract_last(jnp.concatenate(columns, axis=1), jnp.concatenate(lane_hots, axis=1))
    total = both[0:320] + both[320:640]

    def store(v):
        return pltpu.make_async_copy(made.at[v], out_ref.at[v], out_sems.at[v])

    for v in range(5):
        for x in range(8):
            row = v * 64 + x * 8
            top = slice(x * 16, x * 16 + 8)
            bottom = slice(x * 16 + 8, x * 16 + 16)
            made[v, top, :] = base_ref[v, top, :] + total[row : row + 8, 0:128]
            made[v, bottom, :] = base_ref[v, bottom, :] + total[row : row + 8, 128:256]
        for j, y in enumerate((0, 1, 14, 15)):
            rows = pl.ds(y, 8, stride=16)
            made[v, rows, :] = made[v, rows, :] + fix_ref[v, j]
        store(v).start()
    for v in range(5):
        store(v).wait()


def redistribute(helpers, weights, lhs, val, cells, base, fix):
    return pl.pallas_call(
        mix_kernel,
        out_shape=jax.ShapeDtypeStruct(base.shape, F32),
        in_specs=[ANY_SPEC] + [VMEM_SPEC] * 6,
        out_specs=ANY_SPEC,
        scratch_shapes=[
            pltpu.SMEM((32,), jnp.int32),
            pltpu.VMEM((5, 128, 128), F32),
            pltpu.SemaphoreType.DMA,
            pltpu.SemaphoreType.DMA((5,)),
        ],
        compiler_params=PARAMS,
        name="mix_scatter",
    )(helpers, weights, lhs, val, cells, base, fix)


def local(dens_pres, velocity, cut_class, nbhd_cells, helper_list, live_counts, redist_weights):
    ngx, ngy = lax.axis_size("gx"), lax.axis_size("gy")
    dens_pres = dens_pres.reshape(2, 128, 128)
    velocity = velocity.reshape(3, 128, 128)
    cut_class = cut_class.reshape(128, 128)
    packed = pack_weights(redist_weights[0, 0])
    weights = lax.all_to_all(
        packed,
        "gy",
        split_axis=0,
        concat_axis=0,
        axis_index_groups=[columns_in_order(ngy)],
        tiled=True,
    )
    xhead, xtail, yhead, ytail = pack_halo(dens_pres, velocity)
    up_x = [(i, (i + 1) % ngx) for i in range(ngx)]
    up_y = [(i, (i + 1) % ngy) for i in range(ngy)]
    ylo = lax.ppermute(ytail, "gy", up_y)
    yhi = lax.ppermute(yhead, "gy", [(b, a) for a, b in up_y])
    xlo = lax.ppermute(xtail, "gx", up_x)
    xhi = lax.ppermute(xhead, "gx", [(b, a) for a, b in up_x])
    helpers = helper_list[0, 0]
    slots = helpers.shape[0]
    same = helpers[None, :] == helpers[:, None]
    below = lax.broadcasted_iota(jnp.int32, (slots, slots), 1) < lax.broadcasted_iota(
        jnp.int32, (slots, slots), 0
    )
    ranks = jnp.sum((same & below).astype(jnp.int32), axis=1)
    cells = nbhd_cells.reshape(8, 256)
    base, part, edge, scale, half, live = fluxes(
        ranks, live_counts[0], dens_pres, velocity, cut_class, xlo, xhi, cells
    )
    fix, val, lhs = edges(half, live, edge, scale, ylo, yhi, cells, part)
    out = redistribute(helpers, weights, lhs, val, cells, base, fix)
    return out.reshape(5, 8, 16, 128)


def solution(mesh):
    in_specs = (
        P(None, "gx", "gy", None),
        P(None, "gx", "gy", None),
        P("gx", "gy", None),
        P("gx", "gy", None, None),
        P("gx", "gy", None),
        P("gx", "gy"),
        P("gx", "gy", None, None, None, None),
    )
    out_specs = P(None, "gx", "gy", None)
    return jax.shard_map(local, mesh=mesh, in_specs=in_specs, out_specs=out_specs, check_vma=False)
```

```python
import jax
import jax.numpy as jnp
from jax import lax
from jax.experimental import pallas as pl
from jax.experimental.pallas import tpu as pltpu
from jax.sharding import PartitionSpec as P

GAS_GAMMA = 1.4
STEP_RATIO = 0.3
F32 = jnp.float32
BF16 = jnp.bfloat16
VMEM_SPEC = pl.BlockSpec(memory_space=pltpu.VMEM)
SMEM_SPEC = pl.BlockSpec(memory_space=pltpu.SMEM)
ANY_SPEC = pl.BlockSpec(memory_space=pl.ANY)
PARAMS = pltpu.CompilerParams(vmem_limit_bytes=16 << 20)


def comp_ref(dp_ref, vel_ref, comp):
    return (vel_ref, comp - 1) if 1 <= comp <= 3 else (dp_ref, comp // 4)


def halo_kernel(dp_ref, vel_ref, xhead_ref, xtail_ref, yhead_ref, ytail_ref):
    for comp in range(5):
        ref, k = comp_ref(dp_ref, vel_ref, comp)
        xhead_ref[comp] = ref[k, 0:32, :]
        xtail_ref[comp] = ref[k, 96:128, :]
        for j in range(2):
            row = comp * 16 + j * 8
            yhead_ref[row : row + 8, :] = ref[k, pl.ds(j, 8, stride=16), :]
            ytail_ref[row : row + 8, :] = ref[k, pl.ds(14 + j, 8, stride=16), :]


def pack_halo(dens_pres, velocity):
    xs = jax.ShapeDtypeStruct((5, 32, 128), F32)
    ys = jax.ShapeDtypeStruct((80, 128), F32)
    return pl.pallas_call(
        halo_kernel,
        out_shape=(xs, xs, ys, ys),
        in_specs=[VMEM_SPEC] * 2,
        out_specs=(VMEM_SPEC,) * 4,
        compiler_params=PARAMS,
        name="halo_pack",
    )(dens_pres, velocity)


def place_of(g):
    x, z = g >> 3, g & 7
    return (7 - z) * 4 + (x)


def columns_in_order(count):
    return sorted(range(count), key=place_of)


def weight_kernel(w_ref, o_ref, held, packed, in_sems, out_sems):
    chunks = in_sems.shape[0]
    depth = w_ref.shape[1] // chunks
    step = w_ref.shape[0] * depth
    order = columns_in_order(chunks * step)

    def load(c):
        part = pl.ds((chunks - 1 - c) * depth, depth)
        return pltpu.make_async_copy(w_ref.at[:, part], held.at[:, part], in_sems.at[c])

    def store(c):
        part = pl.ds(c * step, step)
        return pltpu.make_async_copy(packed.at[part], o_ref.at[part], out_sems.at[c])

    for c in range(chunks):
        load(c).start()
    for c in range(chunks):
        load(c).wait()
        for k in range(c * step, (c + 1) * step):
            x, z = order[k] >> 3, order[k] & 7
            packed[k] = jnp.concatenate([held[x, z, 0], held[x, z, 1]], axis=-1)
        store(c).start()
    for c in range(chunks):
        store(c).wait()


def pack_weights(weights):
    blocks, cap, n, _ = weights.shape
    weights = weights.reshape(4, 8, cap, n, n)
    return pl.pallas_call(
        weight_kernel,
        out_shape=jax.ShapeDtypeStruct((blocks, n, cap * n), F32),
        in_specs=[ANY_SPEC],
        out_specs=ANY_SPEC,
        scratch_shapes=[
            pltpu.VMEM(weights.shape, F32),
            pltpu.VMEM((blocks, n, cap * n), F32),
            pltpu.SemaphoreType.DMA((4,)),
            pltpu.SemaphoreType.DMA((4,)),
        ],
        compiler_params=pltpu.CompilerParams(vmem_limit_bytes=60 << 20),
        name="weight_pack",
    )(weights)


def minmod(a, b):
    return jnp.maximum(jnp.minimum(a, b), 0.0) + jnp.minimum(jnp.maximum(a, b), 0.0)


def cons_of(p):
    rho, u, v, w, pr = p
    ke = u * u + v * v + w * w
    return [rho, rho * u, rho * v, rho * w, pr * (1.0 / (GAS_GAMMA - 1.0)) + 0.5 * rho * ke]


def face_parts(p, n):
    cons = cons_of(p)
    un, pr = p[1 + n], p[4]
    flux = [c * un for c in cons]
    flux[1 + n] = flux[1 + n] + pr
    flux[4] = flux[4] + pr * un
    gp = GAS_GAMMA * pr
    speed = jnp.abs(un) + gp * lax.rsqrt(gp * p[0])
    return cons, flux, speed


def rusanov2(low, up, n):
    c0, f0, s0 = face_parts(low, n)
    c1, f1, s1 = face_parts(up, n)
    wave = jnp.maximum(s0, s1)
    return [(f0[i] + f1[i]) - wave * (c1[i] - c0[i]) for i in range(5)]


def rolled_divergence(p, axis, n, keep=None):
    length = p[0].shape[axis]

    def back(v):
        return pltpu.roll(v, 1, axis)

    def ahead(v):
        return pltpu.roll(v, length - 1, axis)

    low, up = [], []
    for v in p:
        d = v - back(v)
        half = 0.5 * minmod(d, ahead(d))
        low.append(v + half)
        up.append(ahead(v - half))
    flux = rusanov2(low, up, n)
    if keep is not None:
        flux = [jnp.where(keep, f, 0.0) for f in flux]
    return [f - back(f) for f in flux]


def cell_parts(c):
    row = (c >> 11) * 8 + ((c >> 7) & 7)
    lane = ((c >> 10) & 1) * 128 + (c & 127)
    return row, lane


def one_hot(ids, size):
    width = ids.shape[1]
    return lax.broadcasted_iota(jnp.int32, (size, width), 0) == ids


def two_parts(v):
    hi = v.astype(BF16)
    return hi, (v - hi.astype(F32)).astype(BF16)


def flux_kernel(
    rank_ref, live_ref, dp_ref, vel_ref, cut_ref, xlo_ref, xhi_ref, cell_ref,
    base_ref, val_ref, edge_ref, scale_ref, half_ref, live_out_ref, xe, dl,
):
    for s in range(32):
        half_ref[s : s + 1, :] = jnp.full((1, 128), rank_ref[s], jnp.int32)
    slot = lax.broadcasted_iota(jnp.int32, (8, 256), 0) * 4
    slot = slot + lax.broadcasted_iota(jnp.int32, (8, 256), 1) // 64
    live_out_ref[...] = jnp.where(slot < live_ref[0], 1.0, 0.0)
    for comp in range(5):
        ref, k = comp_ref(dp_ref, vel_ref, comp)
        xe[comp, 0:32] = xlo_ref[comp]
        xe[comp, 32:160] = ref[k]
        xe[comp, 160:192] = xhi_ref[comp]
        for j, row in enumerate((0, 1, 2, 13, 14, 15)):
            edge_ref[comp, j] = ref[k, pl.ds(row, 8, stride=16), :]
    for j, row in enumerate((0, 1, 14, 15)):
        cut = cut_ref[pl.ds(row, 8, stride=16), :].astype(F32)
        scale_ref[j] = (-2.0 * STEP_RATIO) / (1.0 + cut)

    def plane(j):
        return [xe[c, pl.ds(pl.multiple_of(j * 16, 16), 16), :] for c in range(5)]

    def face_x(j):
        a, b, c, d = plane(j - 1), plane(j), plane(j + 1), plane(j + 2)
        low, up = [], []
        for i in range(5):
            mid = c[i] - b[i]
            low.append(b[i] + 0.5 * minmod(b[i] - a[i], mid))
            up.append(c[i] - 0.5 * minmod(mid, d[i] - c[i]))
        return rusanov2(low, up, 0)

    row_id = lax.broadcasted_iota(jnp.int32, (16, 128), 0)
    inner = (row_id >= 1) & (row_id <= 13)

    def body(x, before):
        after = face_x(x + 2)
        centre = plane(x + 2)
        ydiv = rolled_divergence(centre, 0, 1, inner)
        zdiv = rolled_divergence(centre, 1, 2)
        here = pl.ds(pl.multiple_of(x * 16, 16), 16)
        scale = (-2.0 * STEP_RATIO) / (1.0 + cut_ref[here, :].astype(F32))
        cons = cons_of(centre)
        for i in range(5):
            delta = scale * ((after[i] - before[i]) + zdiv[i] + ydiv[i])
            base_ref[i, here, :] = cons[i] + delta
            row = pl.multiple_of(i * 64 + x * 8, 8)
            dl[pl.ds(row, 8), 0:128] = delta[0:8]
            dl[pl.ds(row, 8), 128:256] = delta[8:16]
        return after

    lax.fori_loop(0, 8, body, face_x(1))

    whole = dl[...]
    hi = whole.astype(BF16)
    rest = whole - hi.astype(F32)
    mid, low = two_parts(rest)
    pieces = jnp.concatenate([hi, mid, low], axis=0)
    for q in range(8):
        row, lane = cell_parts(cell_ref[q : q + 1, :])
        lane_hot = one_hot(lane, 256).astype(F32).astype(BF16)
        got = jnp.dot(pieces, lane_hot, preferred_element_type=F32)
        got = got[0:320] + (got[320:640] + got[640:960])
        row_hot = one_hot(row, 64)
        rows = [
            jnp.sum(jnp.where(row_hot, got[v * 64 : v * 64 + 64], 0.0), axis=0, keepdims=True)
            for v in range(5)
        ]
        val_ref[q] = jnp.concatenate(rows + [jnp.zeros((3, 256), F32)], axis=0)


def fluxes(ranks, live, dens_pres, velocity, cut_class, xlo, xhi, cells):
    return pl.pallas_call(
        flux_kernel,
        out_shape=(
            jax.ShapeDtypeStruct((5, 128, 128), F32),
            jax.ShapeDtypeStruct((8, 8, 256), F32),
            jax.ShapeDtypeStruct((5, 6, 8, 128), F32),
            jax.ShapeDtypeStruct((4, 8, 128), F32),
            jax.ShapeDtypeStruct((32, 128), jnp.int32),
            jax.ShapeDtypeStruct((8, 256), F32),
        ),
        in_specs=[SMEM_SPEC] * 2 + [VMEM_SPEC] * 6,
        out_specs=(VMEM_SPEC,) * 6,
        scratch_shapes=[pltpu.VMEM((5, 192, 128), F32), pltpu.VMEM((320, 256), F32)],
        compiler_params=PARAMS,
        name="flux_gather",
    )(ranks, live, dens_pres, velocity, cut_class, xlo, xhi, cells)


def edge_values(half_ref, live_ref, edge_ref, scale_ref, ylo_ref, yhi_ref, cell_ref, part_ref):
    def halo(ref, j):
        return [ref[c * 16 + j * 8 : c * 16 + j * 8 + 8, :] for c in range(5)]

    def own(j):
        return [edge_ref[c, j] for c in range(5)]

    def two_faces(rows):
        low, up = [], []
        for k in (1, 2, 3):
            half = [
                0.5 * minmod(rows[k][c] - rows[k - 1][c], rows[k + 1][c] - rows[k][c])
                for c in range(5)
            ]
            low.append([rows[k][c] + half[c] for c in range(5)])
            up.append([rows[k][c] - half[c] for c in range(5)])
        return rusanov2(low[0], up[1], 1), rusanov2(low[1], up[2], 1)

    face_a, face_b = two_faces([halo(ylo_ref, 0), halo(ylo_ref, 1), own(0), own(1), own(2)])
    face_c, face_d = two_faces([own(3), own(4), own(5), halo(yhi_ref, 0), halo(yhi_ref, 1)])
    fix = []
    for c in range(5):
        fix.append(
            [
                scale_ref[0] * (face_b[c] - face_a[c]),
                -scale_ref[1] * face_b[c],
                scale_ref[2] * face_c[c],
                scale_ref[3] * (face_d[c] - face_c[c]),
            ]
        )
    table = jnp.concatenate(
        [
            jnp.concatenate([fix[c][j], fix[c][j + 2]], axis=1)
            for c in range(5)
            for j in range(2)
        ],
        axis=0,
    )
    pieces = jnp.concatenate(two_parts(table), axis=0)
    half_id = lax.broadcasted_iota(jnp.int32, (8, 128), 1) // 64
    vals, operands, lane_hots = [], [], []
    for q in range(8):
        cell = cell_ref[q : q + 1, :]
        x, y, z = cell >> 11, (cell >> 7) & 15, cell & 127
        on_edge = (y < 2) | (y > 13)
        row = jnp.where(on_edge, (y & 1) * 8 + x, -1)
        lane = (y >> 3) * 128 + z
        lane_hots.append(one_hot(lane, 256).astype(F32).astype(BF16))
        got = jnp.dot(pieces, lane_hots[q], preferred_element_type=F32)
        got = got[0:80] + got[80:160]
        row_hot = one_hot(row, 16)
        rows = [
            jnp.sum(jnp.where(row_hot, got[c * 16 : c * 16 + 16], 0.0), axis=0, keepdims=True)
            for c in range(5)
        ]
        val = part_ref[q] + jnp.concatenate(rows + [jnp.zeros((3, 256), F32)], axis=0)
        val = jnp.where(live_ref[q : q + 1, :] > 0.0, val, 0.0)
        vals.append(val)
        placed = []
        for t in range(4):
            piece = val[:, (t // 2) * 128 : (t // 2) * 128 + 128]
            rank = half_ref[q * 4 + t : q * 4 + t + 1, :]
            moved = jnp.where(rank == t % 2, piece, pltpu.roll(piece, 64, 1))
            placed.append(jnp.where(half_id == rank, moved, 0.0))
        both = jnp.concatenate(two_parts(jnp.concatenate(placed, axis=0)), axis=0)
        operands.append(jnp.concatenate([both, both], axis=1))
    return fix, vals, operands, lane_hots


def contract_last(a, b):
    return lax.dot_general(a, b, (((1,), (1,)), ((), ())), preferred_element_type=F32)


def mix_kernel(
    helper_ref, w_ref, half_ref, live_ref, edge_ref, scale_ref, ylo_ref, yhi_ref, cell_ref, part_ref,
    base_ref, out_ref, helper, made, helper_sem, out_sems,
):
    fetch = pltpu.make_async_copy(helper_ref, helper, helper_sem)
    fetch.start()
    fix, vals, operands, lane_hots = edge_values(
        half_ref, live_ref, edge_ref, scale_ref, ylo_ref, yhi_ref, cell_ref, part_ref
    )
    slot_of = lax.broadcasted_iota(jnp.int32, (8, 256), 1) // 64
    row_hots = [one_hot(cell_parts(cell_ref[q : q + 1, :])[0], 64) for q in range(8)]
    fetch.wait()
    diffs = []
    for q in range(8):
        tiles = []
        for t in range(4):
            w_hi, w_lo = two_parts(w_ref[place_of(helper[q * 4 + t])])
            tiles.append(jnp.concatenate([w_hi, w_lo], axis=1))
        got = contract_last(operands[q], jnp.concatenate(tiles, axis=0))
        got = got[0:32] + got[32:64]
        mixed = got[0:8]
        for t in range(1, 4):
            mixed = jnp.where(slot_of == t, got[t * 8 : t * 8 + 8], mixed)
        diffs.append(mixed - vals[q])
    columns = []
    for q in range(8):
        d_hi = diffs[q].astype(BF16).astype(F32)
        spread = [
            jnp.where(row_hots[q], d[v : v + 1, :], 0.0).astype(BF16)
            for d in (d_hi, diffs[q] - d_hi)
            for v in range(5)
        ]
        columns.append(jnp.concatenate(spread, axis=0))
    both = contract_last(jnp.concatenate(columns, axis=1), jnp.concatenate(lane_hots, axis=1))
    total = both[0:320] + both[320:640]

    def store(v):
        return pltpu.make_async_copy(made.at[v], out_ref.at[v], out_sems.at[v])

    for v in range(5):
        for x in range(8):
            row = v * 64 + x * 8
            top = slice(x * 16, x * 16 + 8)
            bottom = slice(x * 16 + 8, x * 16 + 16)
            made[v, top, :] = base_ref[v, top, :] + total[row : row + 8, 0:128]
            made[v, bottom, :] = base_ref[v, bottom, :] + total[row : row + 8, 128:256]
        for j, y in enumerate((0, 1, 14, 15)):
            rows = pl.ds(y, 8, stride=16)
            made[v, rows, :] = made[v, rows, :] + fix[v][j]
        store(v).start()
    for v in range(5):
        store(v).wait()


def redistribute(helpers, weights, half, live, edge, scale, ylo, yhi, cells, part, base):
    return pl.pallas_call(
        mix_kernel,
        out_shape=jax.ShapeDtypeStruct(base.shape, F32),
        in_specs=[ANY_SPEC] + [VMEM_SPEC] * 10,
        out_specs=ANY_SPEC,
        scratch_shapes=[
            pltpu.SMEM((32,), jnp.int32),
            pltpu.VMEM((5, 128, 128), F32),
            pltpu.SemaphoreType.DMA,
            pltpu.SemaphoreType.DMA((5,)),
        ],
        compiler_params=PARAMS,
        name="mix_scatter",
    )(helpers, weights, half, live, edge, scale, ylo, yhi, cells, part, base)


def local(dens_pres, velocity, cut_class, nbhd_cells, helper_list, live_counts, redist_weights):
    ngx, ngy = lax.axis_size("gx"), lax.axis_size("gy")
    dens_pres = dens_pres.reshape(2, 128, 128)
    velocity = velocity.reshape(3, 128, 128)
    cut_class = cut_class.reshape(128, 128)
    packed = pack_weights(redist_weights[0, 0])
    weights = lax.all_to_all(
        packed,
        "gy",
        split_axis=0,
        concat_axis=0,
        axis_index_groups=[columns_in_order(ngy)],
        tiled=True,
    )
    xhead, xtail, yhead, ytail = pack_halo(dens_pres, velocity)
    up_x = [(i, (i + 1) % ngx) for i in range(ngx)]
    up_y = [(i, (i + 1) % ngy) for i in range(ngy)]
    ylo = lax.ppermute(ytail, "gy", up_y)
    yhi = lax.ppermute(yhead, "gy", [(b, a) for a, b in up_y])
    xlo = lax.ppermute(xtail, "gx", up_x)
    xhi = lax.ppermute(xhead, "gx", [(b, a) for a, b in up_x])
    helpers = helper_list[0, 0]
    slots = helpers.shape[0]
    same = helpers[None, :] == helpers[:, None]
    below = lax.broadcasted_iota(jnp.int32, (slots, slots), 1) < lax.broadcasted_iota(
        jnp.int32, (slots, slots), 0
    )
    ranks = jnp.sum((same & below).astype(jnp.int32), axis=1)
    cells = nbhd_cells.reshape(8, 256)
    base, part, edge, scale, half, live = fluxes(
        ranks, live_counts[0], dens_pres, velocity, cut_class, xlo, xhi, cells
    )
    out = redistribute(
        helpers, weights, half, live, edge, scale, ylo, yhi, cells, part, base
    )
    return out.reshape(5, 8, 16, 128)


def solution(mesh):
    in_specs = (
        P(None, "gx", "gy", None),
        P(None, "gx", "gy", None),
        P("gx", "gy", None),
        P("gx", "gy", None, None),
        P("gx", "gy", None),
        P("gx", "gy"),
        P("gx", "gy", None, None, None, None),
    )
    out_specs = P(None, "gx", "gy", None)
    return jax.shard_map(local, mesh=mesh, in_specs=in_specs, out_specs=out_specs, check_vma=False)
```
